256 devices in a mesh: pack: 32 (over y, z), hist: 8 (over x, core).
Axes of the slice: x: 4, y: 4, z: 8, core: 2. Of those that a mesh axis runs over, the one named last changes fastest.
Arguments:
- queries: bfloat16 [32, 4096, 2048], P('pack', 'hist'), may hold values from -0.59765625 to 0.59765625
- keys: bfloat16 [32, 4096, 2048], P('pack', 'hist'), may hold values from -6 to 6
- values: bfloat16 [32, 4096, 2048], P('pack', 'hist'), may hold values from -6 to 6
- gates: bfloat16 [32, 4096, 2048], P('pack', 'hist'), may hold values from -6 to 6
- user_ids: int32 [32, 4096], P('pack', 'hist'), may hold values from 0 to 5, never falling along the last dimension, each value on 1 to 1365 neighbouring positions
- forget_rate: float32 [16], replicated, may hold values from 0.0001 to 0.02
- norm_gain: float32 [2048], replicated, may hold values from 0.1 to 1.9
- w_out: bfloat16 [2048, 2048], P('pack'), may hold values from -0.125 to 0.125
Outputs:
- mixed: bfloat16 [32, 4096, 2048], P('pack', 'hist')
The draws below stay inside these ranges and needn't reach their ends.
Inputs may be any that keep to these rules, and one draw needn't show every extreme that they name: `user_ids`: in each window user ids never fall along the events; each user holds 1 to 1365 consecutive events, and one user exactly 1365.
All inputs are finite; a program needn't handle non-finite values.
Results may differ from the reference program's by a relative error of at most 0.0061.
Values may be sent and summed in bfloat16 or wider, within the bound.
No kernel may reach another device: no remote copies, remote signals or barrier semaphores. Data moves between devices by JAX's collectives and lax.ppermute only.
A program may use at most 128 MiB of HBM per device.

```python
import math
import jax
import jax.numpy as jnp
import numpy as np
from jax import lax

D = 2048
HEADS = 16
HEAD_DIM = 128
GROUP = 128
USERS = 6
EVENTS = 4096
LONGEST = 1365
WINDOWS = 32


def block_levels(own_key, shape, cuts, smallest, high):
    level, own = 1.0, jax.random.fold_in(own_key, 6)
    for dim, blocks in cuts:
        draws = jnp.exp(jax.random.uniform(jax.random.fold_in(own, dim), (blocks,), jnp.float32, smallest / len(cuts), high / len(cuts)))
        level = level * jnp.repeat(draws, shape[dim] // blocks).reshape([-1 if axis == dim else 1 for axis in range(len(shape))])
    return level


def profile(amount, total, most, slope):
    loads = [(1 << 20) // math.isqrt(rank ** slope) + 1 for rank in range(2, amount + 1)]
    rest, given = total - most - (amount - 1), [1] * (amount - 1)
    while rest > 0:
        movable = [i for i in range(amount - 1) if given[i] < most]
        whole, budget = sum([loads[i] for i in movable]), rest
        for i in movable:
            extra = min(most - given[i], max(1, budget * loads[i] // whole), rest)
            given[i] = given[i] + extra
            rest = rest - extra
    return np.array([most] + given)


def ragged(stream_key, number_of, total, most, slope):
    if number_of == 2:
        one = jax.random.randint(stream_key, (), max(1, total - most), min(most, total - 1) + 1)
        return jnp.stack([one, total - one])
    sizes = jnp.asarray(profile(number_of, total, most, slope), jnp.int32)
    couples = (number_of - 1) // 2
    giver, receiver = sizes[1:1 + 2 * couples:2], sizes[2:2 + 2 * couples:2]
    slack = jnp.minimum(giver - 1, most - receiver)
    shifted = jax.random.randint(jax.random.fold_in(stream_key, 1), (couples,), 0, 1 << 20) % (slack + 1)
    sizes = sizes.at[1:1 + 2 * couples:2].set(giver - shifted).at[2:2 + 2 * couples:2].set(receiver + shifted)
    return sizes[jax.random.permutation(jax.random.fold_in(stream_key, 2), number_of)]


def bell_draw(key, shape, deviation, most, split=(), kind=jnp.bfloat16):
    entries = jax.random.normal(key, shape, jnp.float32) * deviation
    if len(split) > 0:
        entries = block_levels(key, shape, split, -0.22, 0.18) * entries
    return jnp.clip(entries, min=-most, max=most).astype(kind)


def setup_inputs(seed: int = 0) -> dict:
    key_list = jax.random.split(jax.random.key(seed), 9)
    queries = bell_draw(key_list[0], (WINDOWS, EVENTS, D), 0.09, 0.59765625, ((0, 32), (1, 8)))
    keys = bell_draw(key_list[1], (WINDOWS, EVENTS, D), 1.0, 6.0, ((0, 32), (1, 8)))
    values = bell_draw(key_list[2], (WINDOWS, EVENTS, D), 1.0, 6.0, ((0, 32), (1, 8)))
    gates = bell_draw(key_list[3], (WINDOWS, EVENTS, D), 1.0, 6.0, ((0, 32), (1, 8)))
    user_ids = jax.vmap(lambda own: jnp.searchsorted(jnp.cumsum(ragged(own, USERS, EVENTS, LONGEST, 2)), jnp.arange(EVENTS), side="right"))(jax.random.split(key_list[4], WINDOWS)).reshape((WINDOWS, EVENTS)).astype(jnp.int32)
    forget_rate = jnp.clip(jnp.exp(jax.random.uniform(key_list[5], (HEADS,), jnp.float32, math.log(0.0001), math.log(0.02))), 0.0001, 0.02)
    norm_gain = jnp.clip(1.0 + 0.18 * jax.random.normal(key_list[6], (D,), jnp.float32), 0.1, 1.9)
    w_out = bell_draw(key_list[7], (D, D), D ** -0.5, 0.125, ((0, 32),))
    return dict(queries=queries, keys=keys, values=values, gates=gates, user_ids=user_ids, forget_rate=forget_rate, norm_gain=norm_gain, w_out=w_out)


def one_window(items, forget_rate, norm_gain, w_out):
    queries, keys, values, gates, user_ids = items
    blocks = EVENTS // GROUP
    log_decay = jnp.log1p(-forget_rate.astype(jnp.float32))
    prior = jnp.concatenate([jnp.full((1,), -1, jnp.int32), user_ids[:-1].astype(jnp.int32)])
    starts = (user_ids != prior).astype(jnp.int32)
    seg = user_ids.reshape(blocks, GROUP)
    start_blk = starts.reshape(blocks, GROUP)
    qf = queries.astype(jnp.float32).reshape(blocks, GROUP, HEADS, HEAD_DIM)
    kf = keys.astype(jnp.float32).reshape(blocks, GROUP, HEADS, HEAD_DIM)
    vf = values.astype(jnp.float32).reshape(blocks, GROUP, HEADS, HEAD_DIM)
    place = jnp.arange(GROUP, dtype=jnp.int32)
    diff = place[:, None] - place[None, :]
    causal = diff >= 0
    lag = jnp.where(causal, diff, 0).astype(jnp.float32)
    decay = jnp.exp(lag[None] * log_decay[:, None, None])
    same = seg[:, :, None] == seg[:, None, :]
    mask = jnp.logical_and(same, causal[None])
    scores = jnp.einsum('nthd,nshd->nhts', qf, kf)
    weights = jnp.where(mask[:, None], scores * decay[None], 0.0).astype(jnp.bfloat16)
    inner = jnp.einsum('nhts,nshd->nthd', weights.astype(jnp.float32), vf)
    last_user = seg[:, -1]
    tail = jnp.exp((GROUP - 1 - place).astype(jnp.float32)[None, :] * log_decay[:, None])
    keep_rows = (seg == last_user[:, None]).astype(jnp.float32)
    scaled = (kf * (keep_rows[:, :, None] * tail.T[None])[..., None]).astype(jnp.bfloat16)
    own = jnp.einsum('nshd,nshe->nhde', scaled.astype(jnp.float32), vf)
    any_start = lax.optimization_barrier(jnp.max(start_blk, axis=1)) > 0
    keep = jnp.where(any_start[:, None], 0.0, jnp.exp(GROUP * log_decay)[None, :])

    def advance(state, item):
        keep_c, own_c = item
        return (keep_c[:, None, None] * state + own_c, state)
    zero_state = jnp.zeros((HEADS, HEAD_DIM, HEAD_DIM), jnp.float32)
    final, entering = lax.scan(advance, zero_state, (keep, own))
    entering = entering.astype(jnp.bfloat16)
    open_run = (jnp.cumsum(start_blk, axis=1) == 0).astype(jnp.float32)
    reach = jnp.exp((place + 1).astype(jnp.float32)[:, None] * log_decay[None, :])
    factor = open_run[:, :, None] * reach[None]
    carried = jnp.einsum('nthd,nhde->nthe', qf, entering.astype(jnp.float32)) * factor[..., None]
    retained = (inner + carried).reshape(EVENTS, HEADS, HEAD_DIM)
    mean = lax.optimization_barrier(jnp.mean(retained, axis=2, keepdims=True))
    centred = retained - mean
    variance = lax.optimization_barrier(jnp.mean(centred * centred, axis=2, keepdims=True))
    normed = (centred * lax.rsqrt(variance + 1e-05)).reshape(EVENTS, D) * norm_gain.astype(jnp.float32)
    gated = (jax.nn.silu(gates.astype(jnp.float32)) * normed).astype(jnp.bfloat16)
    return jnp.dot(gated, w_out, preferred_element_type=jnp.float32).astype(jnp.bfloat16)

def reference(queries, keys, values, gates, user_ids, forget_rate, norm_gain, w_out):

    def per_window(items):
        return one_window(items, forget_rate, norm_gain, w_out)
    return lax.map(per_window, (queries, keys, values, gates, user_ids))
```

```python
import functools

import jax
import jax.numpy as jnp
from jax import lax
from jax.experimental import pallas as pl
from jax.experimental.pallas import tpu as pltpu
from jax.sharding import PartitionSpec as P

HEADS = 16
HEAD = 128
ROWS = 512
HALF = 256
STEP = 4
COLS = STEP * HEAD
WIDTH = 2048
PAYLOAD = WIDTH + 16
NY, NZ, NH = 4, 8, 8
BOTH = ("pack", "hist")
F32 = jnp.float32
BF16 = jnp.bfloat16


def log_decay(rate_ref, h, n=HEAD):
    return jnp.log1p(jnp.full((1, n), -rate_ref[h], F32))


def down_rows(row, rows):
    return jnp.transpose(jnp.broadcast_to(row, (HEAD, rows)))


def state_kernel(rate_ref, u_ref, k_ref, v_ref, pay_ref, mid_ref, mask_ref):
    step = pl.program_id(0)
    u = u_ref[...]

    @pl.when(step == 0)
    def _():
        first, second = u[:, :HALF], u[:, HALF:]
        mask_ref[0] = down_rows((first == u[:, HALF - 1 : HALF]).astype(F32), HALF)
        mask_ref[1] = down_rows((second == u[:, ROWS - 1 :]).astype(F32), HALF)
        pay_ref[WIDTH : WIDTH + 8] = jnp.broadcast_to(u[:, :1].astype(F32), (8, HEAD)).astype(BF16)
        pay_ref[WIDTH + 8 :] = jnp.broadcast_to(u[:, ROWS - 1 :].astype(F32), (8, HEAD)).astype(BF16)

    through = (u[:, HALF - 1 : HALF] == u[:, ROWS - 1 :]).astype(F32)
    left = (HALF - 1 - lax.broadcasted_iota(jnp.int32, (HALF, HEAD), 0)).astype(F32)
    for i in range(STEP):
        ld = log_decay(rate_ref, step * STEP + i)
        tail = jnp.exp(left * ld)
        cols = slice(i * HEAD, (i + 1) * HEAD)
        parts = []
        for b in range(2):
            rows = slice(b * HALF, (b + 1) * HALF)
            scaled = (k_ref[rows, cols].astype(F32) * (mask_ref[b] * tail)).astype(BF16)
            parts.append(
                lax.dot_general(
                    scaled, v_ref[rows, cols], (((0,), (0,)), ((), ())), preferred_element_type=F32
                )
            )
        fade = jnp.exp(jnp.full((1, HEAD), HALF * 1.0, F32) * ld) * through
        mid_ref[i] = parts[0].astype(BF16)
        pay_ref[pl.ds((step * STEP + i) * HEAD, HEAD)] = (parts[1] + fade * parts[0]).astype(BF16)


def inner_kernel(rate_ref, u_ref, q_ref, k_ref, v_ref, mid_ref, out_ref, lag_ref, mask_ref, open_ref):
    step = pl.program_id(0)

    @pl.when(step == 0)
    def _():
        u = u_ref[...]
        t = lax.broadcasted_iota(jnp.int32, (HALF, HALF), 0)
        s = lax.broadcasted_iota(jnp.int32, (HALF, HALF), 1)
        lag_ref[...] = jnp.where(t >= s, t - s, 0).astype(F32)
        for b in range(2):
            across = jnp.broadcast_to(u[:, b * HALF : (b + 1) * HALF], (HALF, HALF))
            down = jnp.transpose(across)
            mask_ref[b] = jnp.where(jnp.logical_and(across == down, t >= s), 1.0, 0.0)
        open_ref[...] = down_rows((u[:, HALF:] == u[:, HALF - 1 : HALF]).astype(F32), HALF)

    past = (1 + lax.broadcasted_iota(jnp.int32, (HALF, HEAD), 0)).astype(F32)
    for i in range(STEP):
        ld = log_decay(rate_ref, step * STEP + i)
        decay = jnp.exp(lag_ref[...] * log_decay(rate_ref, step * STEP + i, HALF))
        cols = slice(i * HEAD, (i + 1) * HEAD)
        for b in range(2):
            rows = slice(b * HALF, (b + 1) * HALF)
            q = q_ref[rows, cols]
            scores = lax.dot_general(
                q, k_ref[rows, cols], (((1,), (1,)), ((), ())), preferred_element_type=F32
            )
            weights = (scores * (decay * mask_ref[b])).astype(BF16)
            inner = jnp.dot(weights, v_ref[rows, cols], preferred_element_type=F32)
            if b == 1:
                carried = jnp.dot(q, mid_ref[i], preferred_element_type=F32)
                inner = inner + carried * (jnp.exp(past * ld) * open_ref[...])
            out_ref[rows, cols] = inner


def pair_kernel(rate_ref, u_ref, own_ref, one_ref, out_ref):
    u = u_ref[...]
    whole = u[:, :1] == u[:, ROWS - 1 :]
    joined = one_ref[WIDTH + 8 : WIDTH + 9].astype(F32) == u[:, :1].astype(F32)
    on = jnp.where(jnp.logical_and(whole, joined), 1.0, 0.0)
    for h in range(HEADS):
        rows = slice(h * HEAD, (h + 1) * HEAD)
        fade = jnp.exp(jnp.full((1, HEAD), ROWS * 1.0, F32) * log_decay(rate_ref, h)) * on
        out_ref[rows] = (own_ref[rows].astype(F32) + fade * one_ref[rows].astype(F32)).astype(BF16)
    out_ref[WIDTH:] = own_ref[WIDTH:]


def gate_kernel(rate_ref, u_ref, one_ref, two_ref, q_ref, part_ref, a_ref, gain_ref, out_ref, open_ref):
    step = pl.program_id(0)
    u = u_ref[...]

    @pl.when(step == 0)
    def _():
        open_ref[...] = down_rows((u == u[:, :1]).astype(F32), ROWS)

    first1 = one_ref[WIDTH : WIDTH + 1].astype(F32)
    last1 = one_ref[WIDTH + 8 : WIDTH + 9].astype(F32)
    last2 = two_ref[WIDTH + 8 : WIDTH + 9].astype(F32)
    near = jnp.where(last1 == u[:, :1].astype(F32), 1.0, 0.0)
    far = jnp.where(jnp.logical_and(first1 == last1, last2 == first1), near, 0.0)
    past = (1 + lax.broadcasted_iota(jnp.int32, (ROWS, HEAD), 0)).astype(F32)
    for i in range(STEP):
        h = step * STEP + i
        ld = log_decay(rate_ref, h)
        cols = slice(i * HEAD, (i + 1) * HEAD)
        rows = pl.ds(pl.multiple_of(h * HEAD, HEAD), HEAD)
        fade = jnp.exp(jnp.full((1, HEAD), ROWS * 1.0, F32) * ld) * far
        state = near * one_ref[rows].astype(F32) + fade * two_ref[rows].astype(F32)
        carried = jnp.dot(q_ref[:, cols], state.astype(BF16), preferred_element_type=F32)
        kept = part_ref[:, cols] + carried * (jnp.exp(past * ld) * open_ref[...])
        mean = jnp.mean(kept, axis=1, keepdims=True)
        centred = kept - mean
        variance = jnp.mean(centred * centred, axis=1, keepdims=True)
        normed = centred * lax.rsqrt(variance + 1e-05) * gain_ref[:, cols]
        a = a_ref[:, cols].astype(F32)
        out_ref[:, cols] = (a / (1.0 + jnp.exp(-a)) * normed).astype(BF16)


def shard_of(way, oc, y, z):
    (y0, z0), (y1, z1) = way
    dy, dz = y0 * (1 - oc) + y1 * oc, z0 * (1 - oc) + z1 * oc
    return ((y + dy + 2 * NY) % NY) * NZ + (z + dz + 2 * NZ) % NZ


def project_kernel(owner, g_ref, *refs):
    pieces, (out_ref, w_ref) = refs[:5], refs[-2:]
    pack = lax.axis_index("pack")
    core = lax.axis_index("hist") % 2
    oc = core if owner == 0 else 1 - core
    y, z = pack // NZ, pack % NZ
    step = pl.program_id(0)

    @pl.when(step == 0)
    def _():
        for piece, ways in zip(pieces, SHARDS):
            for j, way in enumerate(ways):
                rows = pl.ds(pl.multiple_of(shard_of(way, oc, y, z) * 64, 64), 64)
                w_ref[rows] = piece[j * 64 : j * 64 + 64]

    cols = pl.ds(pl.multiple_of(step * 512, 512), 512)
    out_ref[...] = jnp.dot(g_ref[...], w_ref[:, cols], preferred_element_type=F32).astype(BF16)


SMALL = [
    [(0, 0), (0, -4), (-2, 0), (-2, -4), (-1, 0), (-1, -4), (-3, 0), (-3, -4)],
    [(0, 0), (0, -4), (0, -2), (0, 2), (0, -1), (0, -5), (0, -3), (0, 1)],
]


def turned(d):
    return [((y0, z0 + d), (y1 + d, z1)) for (y0, z0), (y1, z1) in zip(*SMALL)]


SHARDS = [turned(0), turned(-1), turned(1), turned(-2)[:4], turned(2)[4:]]


def moves(*ways):
    pairs = []
    for y in range(NY):
        for z in range(NZ):
            for h in range(NH):
                dy, dz = ways[h % 2]
                to = ((y + dy) % NY) * NZ + (z + dz) % NZ
                pairs.append(((y * NZ + z) * NH + h, to * NH + h))
    return pairs


def send(x, *ways):
    return lax.ppermute(x, BOTH, moves(*ways))


def swapped(x):
    return lax.ppermute(x, BOTH, [(i, i ^ 1) for i in range(NY * NZ * NH)])


def gather_first(w):
    core = lax.axis_index("hist") % 2
    x = lax.dynamic_slice_in_dim(w, core * 1024, 1024, 1)
    return x, send(x, (0, 4), (0, 4)), send(x, (2, 0), (0, 2)), send(x, (2, 4), (0, -2))


def gather_second(parts):
    x = jnp.concatenate(parts, 0)
    return x, send(x, (1, 0), (0, 1))


def gather_third(parts):
    x = jnp.concatenate(parts, 0)
    return x, send(x, (0, 1), (1, 0)), send(x, (0, -1), (-1, 0))


def gather_fourth(x, a, b):
    return x, a, b, send(a[:256], (0, 1), (1, 0)), send(b[256:], (0, -1), (-1, 0))


def call(kernel, grid, in_specs, out_specs, out_shape, scratch, flops, nbytes, vmem=14, alias=None):
    return pl.pallas_call(
        kernel,
        grid_spec=pltpu.PrefetchScalarGridSpec(
            num_scalar_prefetch=0,
            grid=grid,
            in_specs=in_specs,
            out_specs=out_specs,
            scratch_shapes=scratch,
        ),
        out_shape=out_shape,
        cost_estimate=pl.CostEstimate(flops=flops, transcendentals=0, bytes_accessed=nbytes),
        compiler_params=pltpu.CompilerParams(vmem_limit_bytes=vmem << 20),
        input_output_aliases=alias or {},
    )


def local(queries, keys, values, gates, user_ids, forget_rate, norm_gain, w_out):
    q, k, v, a = (pltpu.with_memory_space_constraint(x[0], pltpu.HBM) for x in (queries, keys, values, gates))
    gain = norm_gain.reshape(1, WIDTH)
    steps = HEADS // STEP
    smem = pl.BlockSpec(memory_space=pltpu.SMEM)
    users = pl.BlockSpec((1, ROWS), lambda i: (0, 0))
    block = pl.BlockSpec((ROWS, COLS), lambda i: (0, i))
    heads = pl.BlockSpec((STEP, HEAD, HEAD), lambda i: (i, 0, 0))
    full = pl.BlockSpec((PAYLOAD, HEAD), lambda i: (0, 0))
    shape = jax.ShapeDtypeStruct
    pay_shape = shape((PAYLOAD, HEAD), BF16)
    mb = 1 << 20

    first = gather_first(w_out)

    own, mid = call(
        state_kernel, (steps,), [smem, users, block, block], (full, heads),
        (pay_shape, shape((HEADS, HEAD, HEAD), BF16)),
        [pltpu.VMEM((2, HALF, HEAD), F32)], 270 * 10**6, 5 * mb,
    )(forget_rate, user_ids, k, v)
    first, own = lax.optimization_barrier((first, own))
    second = gather_second(first)
    one = lax.ppermute(own, "hist", [(i, i + 1) for i in range(NH - 1)])
    part = call(
        inner_kernel, (steps,), [smem, users, block, block, block, heads], block,
        shape((ROWS, WIDTH), F32),
        [pltpu.VMEM((HALF, HALF), F32), pltpu.VMEM((2, HALF, HALF), F32), pltpu.VMEM((HALF, HEAD), F32)],
        1200 * 10**6, 11 * mb,
    )(forget_rate, user_ids, q, k, v, mid)
    third = gather_third(second)
    pieces = gather_fourth(*third)
    others = [swapped(p) for p in pieces]
    pair = call(
        pair_kernel, (1,), [smem, users, full, full], full, pay_shape, [], 10**6, 3 * mb // 2
    )(forget_rate, user_ids, own, one)
    two = lax.ppermute(pair, "hist", [(i, i + 2) for i in range(NH - 2)])
    gated = call(
        gate_kernel, (steps,),
        [smem, users, full, full, block, block, block, pl.BlockSpec((1, COLS), lambda i: (0, i))],
        block, shape((ROWS, WIDTH), BF16), [pltpu.VMEM((ROWS, HEAD), F32)],
        300 * 10**6, 11 * mb,
    )(forget_rate, user_ids, one, two, q, part, a, gain)

    mixed = None
    for owner, got in enumerate((pieces, others)):

        def column(i, owner=owner):
            core = lax.axis_index("hist") % 2
            return 0, 2 * (core if owner == 0 else 1 - core) + i

        mixed = call(
            functools.partial(project_kernel, owner), (2,),
            [pl.BlockSpec(memory_space=pltpu.VMEM)] * 6 + [pl.BlockSpec(memory_space=pl.ANY)] * owner,
            pl.BlockSpec((ROWS, 512), column), shape((ROWS, WIDTH), BF16),
            [pltpu.VMEM((WIDTH, 1024), BF16)],
            2150 * 10**6, 7 * mb, 14, {6: 0} if owner else None,
        )(gated, *got, *([mixed] if owner else []))
    return mixed[None]


def solution(mesh):
    wide = P("pack", "hist", None)
    in_specs = (wide, wide, wide, wide, P("pack", "hist"), P(), P(), P("pack", None))
    return jax.shard_map(local, mesh=mesh, in_specs=in_specs, out_specs=wide, check_vma=False)
```

```python
import functools

import jax
import jax.numpy as jnp
from jax import lax
from jax.experimental import pallas as pl
from jax.experimental.pallas import tpu as pltpu
from jax.sharding import PartitionSpec as P

HEADS = 16
HEAD = 128
ROWS = 512
HALF = 256
STEP = 4
COLS = STEP * HEAD
WIDTH = 2048
PAYLOAD = WIDTH + 16
NY, NZ, NH = 4, 8, 8
BOTH = ("pack", "hist")
F32 = jnp.float32
BF16 = jnp.bfloat16


def log_decay(rate_ref, h, n=HEAD):
    return jnp.log1p(jnp.full((1, n), -rate_ref[h], F32))


def down_rows(row, rows):
    return jnp.transpose(jnp.broadcast_to(row, (HEAD, rows)))


def state_kernel(rate_ref, u_ref, k_ref, v_ref, pay_ref, mid_ref, mask_ref):
    step = pl.program_id(0)
    u = u_ref[...]

    @pl.when(step == 0)
    def _():
        first, second = u[:, :HALF], u[:, HALF:]
        mask_ref[0] = down_rows((first == u[:, HALF - 1 : HALF]).astype(F32), HALF)
        mask_ref[1] = down_rows((second == u[:, ROWS - 1 :]).astype(F32), HALF)
        pay_ref[WIDTH : WIDTH + 8] = jnp.broadcast_to(u[:, :1].astype(F32), (8, HEAD)).astype(BF16)
        pay_ref[WIDTH + 8 :] = jnp.broadcast_to(u[:, ROWS - 1 :].astype(F32), (8, HEAD)).astype(BF16)

    through = (u[:, HALF - 1 : HALF] == u[:, ROWS - 1 :]).astype(F32)
    left = (HALF - 1 - lax.broadcasted_iota(jnp.int32, (HALF, HEAD), 0)).astype(F32)
    for i in range(STEP):
        ld = log_decay(rate_ref, step * STEP + i)
        tail = jnp.exp(left * ld)
        cols = slice(i * HEAD, (i + 1) * HEAD)
        parts = []
        for b in range(2):
            rows = slice(b * HALF, (b + 1) * HALF)
            scaled = (k_ref[rows, cols].astype(F32) * (mask_ref[b] * tail)).astype(BF16)
            parts.append(
                lax.dot_general(
                    scaled, v_ref[rows, cols], (((0,), (0,)), ((), ())), preferred_element_type=F32
                )
            )
        fade = jnp.exp(jnp.full((1, HEAD), HALF * 1.0, F32) * ld) * through
        mid_ref[i] = parts[0].astype(BF16)
        pay_ref[pl.ds((step * STEP + i) * HEAD, HEAD)] = (parts[1] + fade * parts[0]).astype(BF16)


def inner_kernel(rate_ref, u_ref, q_ref, k_ref, v_ref, mid_ref, out_ref, lag_ref, mask_ref, open_ref):
    step = pl.program_id(0)

    @pl.when(step == 0)
    def _():
        u = u_ref[...]
        t = lax.broadcasted_iota(jnp.int32, (HALF, HALF), 0)
        s = lax.broadcasted_iota(jnp.int32, (HALF, HALF), 1)
        lag_ref[...] = jnp.where(t >= s, t - s, 0).astype(F32)
        for b in range(2):
            across = jnp.broadcast_to(u[:, b * HALF : (b + 1) * HALF], (HALF, HALF))
            down = jnp.transpose(across)
            mask_ref[b] = jnp.where(jnp.logical_and(across == down, t >= s), 1.0, 0.0)
        open_ref[...] = down_rows((u[:, HALF:] == u[:, HALF - 1 : HALF]).astype(F32), HALF)

    past = (1 + lax.broadcasted_iota(jnp.int32, (HALF, HEAD), 0)).astype(F32)
    for i in range(STEP):
        ld = log_decay(rate_ref, step * STEP + i)
        decay = jnp.exp(lag_ref[...] * log_decay(rate_ref, step * STEP + i, HALF))
        cols = slice(i * HEAD, (i + 1) * HEAD)
        for b in range(2):
            rows = slice(b * HALF, (b + 1) * HALF)
            q = q_ref[rows, cols]
            scores = lax.dot_general(
                q, k_ref[rows, cols], (((1,), (1,)), ((), ())), preferred_element_type=F32
            )
            weights = (scores * (decay * mask_ref[b])).astype(BF16)
            inner = jnp.dot(weights, v_ref[rows, cols], preferred_element_type=F32)
            if b == 1:
                carried = jnp.dot(q, mid_ref[i], preferred_element_type=F32)
                inner = inner + carried * (jnp.exp(past * ld) * open_ref[...])
            out_ref[rows, cols] = inner


def pair_kernel(rate_ref, u_ref, own_ref, one_ref, out_ref):
    u = u_ref[...]
    whole = u[:, :1] == u[:, ROWS - 1 :]
    joined = one_ref[WIDTH + 8 : WIDTH + 9].astype(F32) == u[:, :1].astype(F32)
    on = jnp.where(jnp.logical_and(whole, joined), 1.0, 0.0)
    for h in range(HEADS):
        rows = slice(h * HEAD, (h + 1) * HEAD)
        fade = jnp.exp(jnp.full((1, HEAD), ROWS * 1.0, F32) * log_decay(rate_ref, h)) * on
        out_ref[rows] = (own_ref[rows].astype(F32) + fade * one_ref[rows].astype(F32)).astype(BF16)
    out_ref[WIDTH:] = own_ref[WIDTH:]


def gate_kernel(rate_ref, u_ref, one_ref, two_ref, q_ref, part_ref, a_ref, gain_ref, out_ref, open_ref):
    step = pl.program_id(0)
    u = u_ref[...]

    @pl.when(step == 0)
    def _():
        open_ref[...] = down_rows((u == u[:, :1]).astype(F32), ROWS)

    first1 = one_ref[WIDTH : WIDTH + 1].astype(F32)
    last1 = one_ref[WIDTH + 8 : WIDTH + 9].astype(F32)
    last2 = two_ref[WIDTH + 8 : WIDTH + 9].astype(F32)
    near = jnp.where(last1 == u[:, :1].astype(F32), 1.0, 0.0)
    far = jnp.where(jnp.logical_and(first1 == last1, last2 == first1), near, 0.0)
    past = (1 + lax.broadcasted_iota(jnp.int32, (ROWS, HEAD), 0)).astype(F32)
    for i in range(STEP):
        h = step * STEP + i
        ld = log_decay(rate_ref, h)
        cols = slice(i * HEAD, (i + 1) * HEAD)
        rows = pl.ds(pl.multiple_of(h * HEAD, HEAD), HEAD)
        fade = jnp.exp(jnp.full((1, HEAD), ROWS * 1.0, F32) * ld) * far
        state = near * one_ref[rows].astype(F32) + fade * two_ref[rows].astype(F32)
        carried = jnp.dot(q_ref[:, cols], state.astype(BF16), preferred_element_type=F32)
        kept = part_ref[:, cols] + carried * (jnp.exp(past * ld) * open_ref[...])
        mean = jnp.mean(kept, axis=1, keepdims=True)
        centred = kept - mean
        variance = jnp.mean(centred * centred, axis=1, keepdims=True)
        normed = centred * lax.rsqrt(variance + 1e-05) * gain_ref[:, cols]
        a = a_ref[:, cols].astype(F32)
        out_ref[:, cols] = (a / (1.0 + jnp.exp(-a)) * normed).astype(BF16)


def shard_of(way, oc, y, z):
    (y0, z0), (y1, z1) = way
    dy, dz = y0 * (1 - oc) + y1 * oc, z0 * (1 - oc) + z1 * oc
    return ((y + dy + 2 * NY) % NY) * NZ + (z + dz + 2 * NZ) % NZ


def project_kernel(owner, g_ref, *refs):
    pieces, (out_ref, w_ref) = refs[:PIECES], refs[-2:]
    pack = lax.axis_index("pack")
    core = lax.axis_index("hist") % 2
    oc = core if owner == 0 else 1 - core
    y, z = pack // NZ, pack % NZ
    step = pl.program_id(0)

    @pl.when(step == 0)
    def _():
        for piece, ways in zip(pieces, SHARDS):
            for j, way in enumerate(ways):
                rows = pl.ds(pl.multiple_of(shard_of(way, oc, y, z) * 64, 64), 64)
                w_ref[rows] = piece[j * 64 : j * 64 + 64]

    cols = pl.ds(pl.multiple_of(step * 512, 512), 512)
    out_ref[...] = jnp.dot(g_ref[...], w_ref[:, cols], preferred_element_type=F32).astype(BF16)


SMALL = [
    [(0, 0), (-1, 0), (0, -4), (-1, -4), (-2, 0), (-3, 0), (-2, -4), (1, -4)],
    [(0, 0), (0, -1), (0, 1), (0, 2), (0, -2), (0, -3), (0, 3), (0, -4)],
]


def turned(d):
    both = [((y0, z0 + d), (y1 + d, z1)) for (y0, z0), (y1, z1) in zip(*SMALL)]
    return both[:4], both[4:]


SHARDS = [*turned(0), *turned(-1), *turned(1), turned(-2)[0], turned(2)[1]]
PIECES = len(SHARDS)


def moves(*ways):
    pairs = []
    for y in range(NY):
        for z in range(NZ):
            for h in range(NH):
                dy, dz = ways[h % 2]
                to = ((y + dy) % NY) * NZ + (z + dz) % NZ
                pairs.append(((y * NZ + z) * NH + h, to * NH + h))
    return pairs


def send(x, *ways):
    return lax.ppermute(x, BOTH, moves(*ways))


def swapped(x):
    return lax.ppermute(x, BOTH, [(i, i ^ 1) for i in range(NY * NZ * NH)])


def gather(w):
    core = lax.axis_index("hist") % 2
    x = lax.dynamic_slice_in_dim(w, core * 1024, 1024, 1)
    a1 = send(x, (1, 0), (0, 1))
    a2 = send(x, (0, 4), (0, -1))
    b1 = send(a1, (1, 0), (0, 1))
    b2 = send(a2, (1, 0), (0, -1))
    c1 = send(b1, (1, 0), (0, 1))
    c2 = send(b2, (1, 0), (0, -1))
    d1 = send(jnp.where(core == 0, a2, c1), (-1, 0), (0, 1))
    one = jnp.concatenate([x, a1, a2, b2], 0)
    two = jnp.concatenate([b1, c1, c2, d1], 0)
    up1 = send(one, (0, 1), (1, 0))
    down1 = send(one, (0, -1), (-1, 0))
    up2 = send(two, (0, 1), (1, 0))
    down2 = send(two, (0, -1), (-1, 0))
    far1 = send(up1, (0, 1), (1, 0))
    far2 = send(down2, (0, -1), (-1, 0))
    return one, two, up1, up2, down1, down2, far1, far2


def call(kernel, grid, in_specs, out_specs, out_shape, scratch, flops, nbytes, vmem=14, alias=None):
    return pl.pallas_call(
        kernel,
        grid_spec=pltpu.PrefetchScalarGridSpec(
            num_scalar_prefetch=0,
            grid=grid,
            in_specs=in_specs,
            out_specs=out_specs,
            scratch_shapes=scratch,
        ),
        out_shape=out_shape,
        cost_estimate=pl.CostEstimate(flops=flops, transcendentals=0, bytes_accessed=nbytes),
        compiler_params=pltpu.CompilerParams(vmem_limit_bytes=vmem << 20),
        input_output_aliases=alias or {},
    )


def local(queries, keys, values, gates, user_ids, forget_rate, norm_gain, w_out):
    q, k, v, a = (pltpu.with_memory_space_constraint(x[0], pltpu.HBM) for x in (queries, keys, values, gates))
    gain = norm_gain.reshape(1, WIDTH)
    steps = HEADS // STEP
    smem = pl.BlockSpec(memory_space=pltpu.SMEM)
    users = pl.BlockSpec((1, ROWS), lambda i: (0, 0))
    block = pl.BlockSpec((ROWS, COLS), lambda i: (0, i))
    heads = pl.BlockSpec((STEP, HEAD, HEAD), lambda i: (i, 0, 0))
    full = pl.BlockSpec((PAYLOAD, HEAD), lambda i: (0, 0))
    shape = jax.ShapeDtypeStruct
    pay_shape = shape((PAYLOAD, HEAD), BF16)
    mb = 1 << 20

    pieces = gather(w_out)
    others = [swapped(p) for p in pieces]
    own, mid = call(
        state_kernel, (steps,), [smem, users, block, block], (full, heads),
        (pay_shape, shape((HEADS, HEAD, HEAD), BF16)),
        [pltpu.VMEM((2, HALF, HEAD), F32)], 270 * 10**6, 5 * mb,
    )(forget_rate, user_ids, k, v)
    one = lax.ppermute(own, "hist", [(i, i + 1) for i in range(NH - 1)])
    part = call(
        inner_kernel, (steps,), [smem, users, block, block, block, heads], block,
        shape((ROWS, WIDTH), F32),
        [pltpu.VMEM((HALF, HALF), F32), pltpu.VMEM((2, HALF, HALF), F32), pltpu.VMEM((HALF, HEAD), F32)],
        1200 * 10**6, 11 * mb,
    )(forget_rate, user_ids, q, k, v, mid)
    pair = call(
        pair_kernel, (1,), [smem, users, full, full], full, pay_shape, [], 10**6, 3 * mb // 2
    )(forget_rate, user_ids, own, one)
    two = lax.ppermute(pair, "hist", [(i, i + 2) for i in range(NH - 2)])
    gated = call(
        gate_kernel, (steps,),
        [smem, users, full, full, block, block, block, pl.BlockSpec((1, COLS), lambda i: (0, i))],
        block, shape((ROWS, WIDTH), BF16), [pltpu.VMEM((ROWS, HEAD), F32)],
        300 * 10**6, 11 * mb,
    )(forget_rate, user_ids, one, two, q, part, a, gain)

    mixed = None
    for owner, got in enumerate((pieces, others)):

        def column(i, owner=owner):
            core = lax.axis_index("hist") % 2
            return 0, 2 * (core if owner == 0 else 1 - core) + i

        mixed = call(
            functools.partial(project_kernel, owner), (2,),
            [pl.BlockSpec(memory_space=pltpu.VMEM)] * (1 + PIECES) + [pl.BlockSpec(memory_space=pl.ANY)] * owner,
            pl.BlockSpec((ROWS, 512), column), shape((ROWS, WIDTH), BF16),
            [pltpu.VMEM((WIDTH, 1024), BF16)],
            2150 * 10**6, 7 * mb, 14, {1 + PIECES: 0} if owner else None,
        )(gated, *got, *([mixed] if owner else []))
    return mixed[None]


def solution(mesh):
    wide = P("pack", "hist", None)
    in_specs = (wide, wide, wide, wide, P("pack", "hist"), P(), P(), P("pack", None))
    return jax.shard_map(local, mesh=mesh, in_specs=in_specs, out_specs=wide, check_vma=False)
```

```python
import functools

import jax
import jax.numpy as jnp
from jax import lax
from jax.experimental import pallas as pl
from jax.experimental.pallas import tpu as pltpu
from jax.sharding import PartitionSpec as P

HEADS = 16
HEAD = 128
ROWS = 512
HALF = 256
STEP = 4
COLS = STEP * HEAD
WIDTH = 2048
PAYLOAD = WIDTH + 16
NY, NZ, NH = 4, 8, 8
BOTH = ("pack", "hist")
F32 = jnp.float32
BF16 = jnp.bfloat16


def log_decay(rate_ref, h, n=HEAD):
    return jnp.log1p(jnp.full((1, n), -rate_ref[h], F32))


def down_rows(row, rows):
    return jnp.transpose(jnp.broadcast_to(row, (HEAD, rows)))


def state_kernel(rate_ref, u_ref, k_ref, v_ref, pay_ref, mid_ref, mask_ref):
    step = pl.program_id(0)
    u = u_ref[...]

    @pl.when(step == 0)
    def _():
        first, second = u[:, :HALF], u[:, HALF:]
        mask_ref[0] = down_rows((first == u[:, HALF - 1 : HALF]).astype(F32), HALF)
        mask_ref[1] = down_rows((second == u[:, ROWS - 1 :]).astype(F32), HALF)
        pay_ref[WIDTH : WIDTH + 8] = jnp.broadcast_to(u[:, :1].astype(F32), (8, HEAD)).astype(BF16)
        pay_ref[WIDTH + 8 :] = jnp.broadcast_to(u[:, ROWS - 1 :].astype(F32), (8, HEAD)).astype(BF16)

    through = (u[:, HALF - 1 : HALF] == u[:, ROWS - 1 :]).astype(F32)
    left = (HALF - 1 - lax.broadcasted_iota(jnp.int32, (HALF, HEAD), 0)).astype(F32)
    for i in range(STEP):
        ld = log_decay(rate_ref, step * STEP + i)
        tail = jnp.exp(left * ld)
        cols = slice(i * HEAD, (i + 1) * HEAD)
        parts = []
        for b in range(2):
            rows = slice(b * HALF, (b + 1) * HALF)
            scaled = (k_ref[rows, cols].astype(F32) * (mask_ref[b] * tail)).astype(BF16)
            parts.append(
                lax.dot_general(
                    scaled, v_ref[rows, cols], (((0,), (0,)), ((), ())), preferred_element_type=F32
                )
            )
        fade = jnp.exp(jnp.full((1, HEAD), HALF * 1.0, F32) * ld) * through
        mid_ref[i] = parts[0].astype(BF16)
        pay_ref[pl.ds((step * STEP + i) * HEAD, HEAD)] = (parts[1] + fade * parts[0]).astype(BF16)


def inner_kernel(base, rate_ref, u_ref, q_ref, k_ref, v_ref, mid_ref, out_ref, lag_ref, mask_ref, open_ref):
    step = pl.program_id(0)

    @pl.when(step == 0)
    def _():
        u = u_ref[...]
        t = lax.broadcasted_iota(jnp.int32, (HALF, HALF), 0)
        s = lax.broadcasted_iota(jnp.int32, (HALF, HALF), 1)
        lag_ref[...] = jnp.where(t >= s, t - s, 0).astype(F32)
        for b in range(2):
            across = jnp.broadcast_to(u[:, b * HALF : (b + 1) * HALF], (HALF, HALF))
            down = jnp.transpose(across)
            mask_ref[b] = jnp.where(jnp.logical_and(across == down, t >= s), 1.0, 0.0)
        open_ref[...] = down_rows((u[:, HALF:] == u[:, HALF - 1 : HALF]).astype(F32), HALF)

    past = (1 + lax.broadcasted_iota(jnp.int32, (HALF, HEAD), 0)).astype(F32)
    for i in range(STEP):
        ld = log_decay(rate_ref, (base + step) * STEP + i)
        decay = jnp.exp(lag_ref[...] * log_decay(rate_ref, (base + step) * STEP + i, HALF))
        cols = slice(i * HEAD, (i + 1) * HEAD)
        for b in range(2):
            rows = slice(b * HALF, (b + 1) * HALF)
            q = q_ref[rows, cols]
            scores = lax.dot_general(
                q, k_ref[rows, cols], (((1,), (1,)), ((), ())), preferred_element_type=F32
            )
            weights = (scores * (decay * mask_ref[b])).astype(BF16)
            inner = jnp.dot(weights, v_ref[rows, cols], preferred_element_type=F32)
            if b == 1:
                carried = jnp.dot(q, mid_ref[i], preferred_element_type=F32)
                inner = inner + carried * (jnp.exp(past * ld) * open_ref[...])
            out_ref[rows, cols] = inner


def pair_kernel(rate_ref, u_ref, own_ref, one_ref, out_ref):
    u = u_ref[...]
    whole = u[:, :1] == u[:, ROWS - 1 :]
    joined = one_ref[WIDTH + 8 : WIDTH + 9].astype(F32) == u[:, :1].astype(F32)
    on = jnp.where(jnp.logical_and(whole, joined), 1.0, 0.0)
    for h in range(HEADS):
        rows = slice(h * HEAD, (h + 1) * HEAD)
        fade = jnp.exp(jnp.full((1, HEAD), ROWS * 1.0, F32) * log_decay(rate_ref, h)) * on
        out_ref[rows] = (own_ref[rows].astype(F32) + fade * one_ref[rows].astype(F32)).astype(BF16)
    out_ref[WIDTH:] = own_ref[WIDTH:]


def gate_kernel(rate_ref, u_ref, one_ref, two_ref, q_ref, part0_ref, part1_ref, a_ref, gain_ref, out_ref, open_ref):
    step = pl.program_id(0)
    u = u_ref[...]

    @pl.when(step == 0)
    def _():
        open_ref[...] = down_rows((u == u[:, :1]).astype(F32), ROWS)

    first1 = one_ref[WIDTH : WIDTH + 1].astype(F32)
    last1 = one_ref[WIDTH + 8 : WIDTH + 9].astype(F32)
    last2 = two_ref[WIDTH + 8 : WIDTH + 9].astype(F32)
    near = jnp.where(last1 == u[:, :1].astype(F32), 1.0, 0.0)
    far = jnp.where(jnp.logical_and(first1 == last1, last2 == first1), near, 0.0)
    past = (1 + lax.broadcasted_iota(jnp.int32, (ROWS, HEAD), 0)).astype(F32)
    for i in range(STEP):
        h = step * STEP + i
        ld = log_decay(rate_ref, h)
        cols = slice(i * HEAD, (i + 1) * HEAD)
        rows = pl.ds(pl.multiple_of(h * HEAD, HEAD), HEAD)
        fade = jnp.exp(jnp.full((1, HEAD), ROWS * 1.0, F32) * ld) * far
        state = near * one_ref[rows].astype(F32) + fade * two_ref[rows].astype(F32)
        carried = jnp.dot(q_ref[:, cols], state.astype(BF16), preferred_element_type=F32)
        part = jnp.where(step < 2, part0_ref[:, cols], part1_ref[:, cols])
        kept = part + carried * (jnp.exp(past * ld) * open_ref[...])
        mean = jnp.mean(kept, axis=1, keepdims=True)
        centred = kept - mean
        variance = jnp.mean(centred * centred, axis=1, keepdims=True)
        normed = centred * lax.rsqrt(variance + 1e-05) * gain_ref[:, cols]
        a = a_ref[:, cols].astype(F32)
        out_ref[:, cols] = (a / (1.0 + jnp.exp(-a)) * normed).astype(BF16)


def shard_of(way, oc, y, z):
    (y0, z0), (y1, z1) = way
    dy, dz = y0 * (1 - oc) + y1 * oc, z0 * (1 - oc) + z1 * oc
    return ((y + dy + 2 * NY) % NY) * NZ + (z + dz + 2 * NZ) % NZ


def project_kernel(owner, g_ref, *refs):
    pieces, (out_ref, w_ref) = refs[:PIECES], refs[-2:]
    pack = lax.axis_index("pack")
    core = lax.axis_index("hist") % 2
    oc = core if owner == 0 else 1 - core
    y, z = pack // NZ, pack % NZ
    step = pl.program_id(0)

    @pl.when(step == 0)
    def _():
        for piece, ways in zip(pieces, SHARDS):
            for j, way in enumerate(ways):
                rows = pl.ds(pl.multiple_of(shard_of(way, oc, y, z) * 64, 64), 64)
                w_ref[rows] = piece[j * 64 : j * 64 + 64]

    cols = pl.ds(pl.multiple_of(step * 512, 512), 512)
    out_ref[...] = jnp.dot(g_ref[...], w_ref[:, cols], preferred_element_type=F32).astype(BF16)


SMALL = [
    [(0, 0), (-1, 0), (0, -4), (-1, -4), (-2, 0), (-3, 0), (-2, -4), (1, -4)],
    [(0, 0), (0, -1), (0, 1), (0, 2), (0, -2), (0, -3), (0, 3), (0, -4)],
]


def turned(d):
    both = [((y0, z0 + d), (y1 + d, z1)) for (y0, z0), (y1, z1) in zip(*SMALL)]
    return both[:4], both[4:]


SHARDS = [*turned(0), *turned(-1), *turned(1), turned(-2)[0], turned(2)[1]]
PIECES = len(SHARDS)


def moves(*ways):
    pairs = []
    for y in range(NY):
        for z in range(NZ):
            for h in range(NH):
                dy, dz = ways[h % 2]
                to = ((y + dy) % NY) * NZ + (z + dz) % NZ
                pairs.append(((y * NZ + z) * NH + h, to * NH + h))
    return pairs


def send(x, *ways):
    return lax.ppermute(x, BOTH, moves(*ways))


def swapped(x):
    return lax.ppermute(x, BOTH, [(i, i ^ 1) for i in range(NY * NZ * NH)])


def gather(w):
    core = lax.axis_index("hist") % 2
    x = lax.dynamic_slice_in_dim(w, core * 1024, 1024, 1)
    a1 = send(x, (1, 0), (0, 1))
    a2 = send(x, (0, 4), (0, -1))
    b1 = send(a1, (1, 0), (0, 1))
    b2 = send(a2, (1, 0), (0, -1))
    c1 = send(b1, (1, 0), (0, 1))
    c2 = send(b2, (1, 0), (0, -1))
    d1 = send(jnp.where(core == 0, a2, c1), (-1, 0), (0, 1))
    one = jnp.concatenate([x, a1, a2, b2], 0)
    two = jnp.concatenate([b1, c1, c2, d1], 0)
    up1 = send(one, (0, 1), (1, 0))
    down1 = send(one, (0, -1), (-1, 0))
    up2 = send(two, (0, 1), (1, 0))
    down2 = send(two, (0, -1), (-1, 0))
    far1 = send(up1, (0, 1), (1, 0))
    far2 = send(down2, (0, -1), (-1, 0))
    return one, two, up1, up2, down1, down2, far1, far2


def call(kernel, grid, in_specs, out_specs, out_shape, scratch, flops, nbytes, vmem=14, alias=None):
    return pl.pallas_call(
        kernel,
        grid_spec=pltpu.PrefetchScalarGridSpec(
            num_scalar_prefetch=0,
            grid=grid,
            in_specs=in_specs,
            out_specs=out_specs,
            scratch_shapes=scratch,
        ),
        out_shape=out_shape,
        cost_estimate=pl.CostEstimate(flops=flops, transcendentals=0, bytes_accessed=nbytes),
        compiler_params=pltpu.CompilerParams(vmem_limit_bytes=vmem << 20),
        input_output_aliases=alias or {},
    )


def local(queries, keys, values, gates, user_ids, forget_rate, norm_gain, w_out):
    q, k, v, a = (pltpu.with_memory_space_constraint(x[0], pltpu.HBM) for x in (queries, keys, values, gates))
    user_ids, forget_rate = (pltpu.with_memory_space_constraint(x, pltpu.HBM) for x in (user_ids, forget_rate))
    gain = norm_gain.reshape(1, WIDTH)
    steps = HEADS // STEP
    smem = pl.BlockSpec(memory_space=pltpu.SMEM)
    users = pl.BlockSpec((1, ROWS), lambda i: (0, 0))
    block = pl.BlockSpec((ROWS, COLS), lambda i: (0, i))
    heads = pl.BlockSpec((STEP, HEAD, HEAD), lambda i: (i, 0, 0))
    full = pl.BlockSpec((PAYLOAD, HEAD), lambda i: (0, 0))
    shape = jax.ShapeDtypeStruct
    pay_shape = shape((PAYLOAD, HEAD), BF16)
    mb = 1 << 20

    pieces = gather(w_out)
    others = [swapped(p) for p in pieces]
    own, mid = call(
        state_kernel, (steps,), [smem, users, block, block], (full, heads),
        (pay_shape, shape((HEADS, HEAD, HEAD), BF16)),
        [pltpu.VMEM((2, HALF, HEAD), F32)], 270 * 10**6, 5 * mb,
    )(forget_rate, user_ids, k, v)
    one = lax.ppermute(own, "hist", [(i, i + 1) for i in range(NH - 1)])
    parts = []
    for i in range(2):

        def at(j, i=i):
            return 0, 2 * i + j

        half = pl.BlockSpec((ROWS, COLS), at)
        mids = pl.BlockSpec((STEP, HEAD, HEAD), lambda j, i=i: (2 * i + j, 0, 0))
        parts.append(
            call(
                functools.partial(inner_kernel, 2 * i), (2,), [smem, users, half, half, half, mids],
                block, shape((ROWS, WIDTH // 2), F32),
                [pltpu.VMEM((HALF, HALF), F32), pltpu.VMEM((2, HALF, HALF), F32), pltpu.VMEM((HALF, HEAD), F32)],
                600 * 10**6, 6 * mb,
            )(forget_rate, user_ids, q, k, v, mid)
        )
    pair = call(
        pair_kernel, (1,), [smem, users, full, full], full, pay_shape, [], 10**6, 3 * mb // 2
    )(forget_rate, user_ids, own, one)
    two = lax.ppermute(pair, "hist", [(i, i + 2) for i in range(NH - 2)])
    gated = call(
        gate_kernel, (steps,),
        [
            smem, users, full, full, block,
            pl.BlockSpec((ROWS, COLS), lambda i: (0, jnp.minimum(i, 1))),
            pl.BlockSpec((ROWS, COLS), lambda i: (0, jnp.maximum(i - 2, 0))),
            block, pl.BlockSpec((1, COLS), lambda i: (0, i)),
        ],
        block, shape((ROWS, WIDTH), BF16), [pltpu.VMEM((ROWS, HEAD), F32)],
        300 * 10**6, 11 * mb,
    )(forget_rate, user_ids, one, two, q, *parts, a, gain)

    mixed = None
    for owner, got in enumerate((pieces, others)):

        def column(i, owner=owner):
            core = lax.axis_index("hist") % 2
            return 0, 2 * (core if owner == 0 else 1 - core) + i

        mixed = call(
            functools.partial(project_kernel, owner), (2,),
            [pl.BlockSpec(memory_space=pltpu.VMEM)] * (1 + PIECES) + [pl.BlockSpec(memory_space=pl.ANY)] * owner,
            pl.BlockSpec((ROWS, 512), column), shape((ROWS, WIDTH), BF16),
            [pltpu.VMEM((WIDTH, 1024), BF16)],
            2150 * 10**6, 7 * mb, 14, {1 + PIECES: 0} if owner else None,
        )(gated, *got, *([mixed] if owner else []))
    return mixed[None]


def solution(mesh):
    wide = P("pack", "hist", None)
    in_specs = (wide, wide, wide, wide, P("pack", "hist"), P(), P(), P("pack", None))
    return jax.shard_map(local, mesh=mesh, in_specs=in_specs, out_specs=wide, check_vma=False)
```

```python
import functools

import jax
import jax.numpy as jnp
from jax import lax
from jax.experimental import pallas as pl
from jax.experimental.pallas import tpu as pltpu
from jax.sharding import PartitionSpec as P

HEADS = 16
HEAD = 128
ROWS = 512
HALF = 256
STEP = 4
COLS = STEP * HEAD
WIDTH = 2048
PAYLOAD = WIDTH + 16
NY, NZ, NH = 4, 8, 8
BOTH = ("pack", "hist")
F32 = jnp.float32
BF16 = jnp.bfloat16


def log_decay(rate_ref, h, n=HEAD):
    return jnp.log1p(jnp.full((1, n), -rate_ref[h], F32))


def down_rows(row, rows):
    return jnp.transpose(jnp.broadcast_to(row, (HEAD, rows)))


def state_kernel(rate_ref, u_ref, k_ref, v_ref, pay_ref, mid_ref, mask_ref):
    step = pl.program_id(0)
    u = u_ref[...]

    @pl.when(step == 0)
    def _():
        first, second = u[:, :HALF], u[:, HALF:]
        mask_ref[0] = down_rows((first == u[:, HALF - 1 : HALF]).astype(F32), HALF)
        mask_ref[1] = down_rows((second == u[:, ROWS - 1 :]).astype(F32), HALF)
        pay_ref[WIDTH : WIDTH + 8] = jnp.broadcast_to(u[:, :1].astype(F32), (8, HEAD)).astype(BF16)
        pay_ref[WIDTH + 8 :] = jnp.broadcast_to(u[:, ROWS - 1 :].astype(F32), (8, HEAD)).astype(BF16)

    through = (u[:, HALF - 1 : HALF] == u[:, ROWS - 1 :]).astype(F32)
    left = (HALF - 1 - lax.broadcasted_iota(jnp.int32, (HALF, HEAD), 0)).astype(F32)
    for i in range(STEP):
        ld = log_decay(rate_ref, step * STEP + i)
        tail = jnp.exp(left * ld)
        cols = slice(i * HEAD, (i + 1) * HEAD)
        parts = []
        for b in range(2):
            rows = slice(b * HALF, (b + 1) * HALF)
            scaled = (k_ref[rows, cols].astype(F32) * (mask_ref[b] * tail)).astype(BF16)
            parts.append(
                lax.dot_general(
                    scaled, v_ref[rows, cols], (((0,), (0,)), ((), ())), preferred_element_type=F32
                )
            )
        fade = jnp.exp(jnp.full((1, HEAD), HALF * 1.0, F32) * ld) * through
        mid_ref[i] = parts[0].astype(BF16)
        pay_ref[pl.ds((step * STEP + i) * HEAD, HEAD)] = (parts[1] + fade * parts[0]).astype(BF16)


def inner_kernel(base, rate_ref, u_ref, q_ref, k_ref, v_ref, mid_ref, out_ref, lag_ref, mask_ref, open_ref):
    step = pl.program_id(0)

    @pl.when(step == 0)
    def _():
        u = u_ref[...]
        t = lax.broadcasted_iota(jnp.int32, (HALF, HALF), 0)
        s = lax.broadcasted_iota(jnp.int32, (HALF, HALF), 1)
        lag_ref[...] = jnp.where(t >= s, t - s, 0).astype(F32)
        for b in range(2):
            across = jnp.broadcast_to(u[:, b * HALF : (b + 1) * HALF], (HALF, HALF))
            down = jnp.transpose(across)
            mask_ref[b] = jnp.where(jnp.logical_and(across == down, t >= s), 1.0, 0.0)
        open_ref[...] = down_rows((u[:, HALF:] == u[:, HALF - 1 : HALF]).astype(F32), HALF)

    past = (1 + lax.broadcasted_iota(jnp.int32, (HALF, HEAD), 0)).astype(F32)
    for i in range(STEP):
        ld = log_decay(rate_ref, (base + step) * STEP + i)
        decay = jnp.exp(lag_ref[...] * log_decay(rate_ref, (base + step) * STEP + i, HALF))
        cols = slice(i * HEAD, (i + 1) * HEAD)
        for b in range(2):
            rows = slice(b * HALF, (b + 1) * HALF)
            q = q_ref[rows, cols]
            scores = lax.dot_general(
                q, k_ref[rows, cols], (((1,), (1,)), ((), ())), preferred_element_type=F32
            )
            weights = (scores * (decay * mask_ref[b])).astype(BF16)
            inner = jnp.dot(weights, v_ref[rows, cols], preferred_element_type=F32)
            if b == 1:
                carried = jnp.dot(q, mid_ref[i], preferred_element_type=F32)
                inner = inner + carried * (jnp.exp(past * ld) * open_ref[...])
            out_ref[rows, cols] = inner


def pair_kernel(rate_ref, u_ref, own_ref, one_ref, out_ref):
    u = u_ref[...]
    whole = u[:, :1] == u[:, ROWS - 1 :]
    joined = one_ref[WIDTH + 8 : WIDTH + 9].astype(F32) == u[:, :1].astype(F32)
    on = jnp.where(jnp.logical_and(whole, joined), 1.0, 0.0)
    for h in range(HEADS):
        rows = slice(h * HEAD, (h + 1) * HEAD)
        fade = jnp.exp(jnp.full((1, HEAD), ROWS * 1.0, F32) * log_decay(rate_ref, h)) * on
        out_ref[rows] = (own_ref[rows].astype(F32) + fade * one_ref[rows].astype(F32)).astype(BF16)
    out_ref[WIDTH:] = own_ref[WIDTH:]


def gate_kernel(rate_ref, u_ref, one_ref, two_ref, q_ref, part0_ref, part1_ref, a_ref, gain_ref, out_ref, open_ref):
    step = pl.program_id(0)
    u = u_ref[...]

    @pl.when(step == 0)
    def _():
        open_ref[...] = down_rows((u == u[:, :1]).astype(F32), ROWS)

    first1 = one_ref[WIDTH : WIDTH + 1].astype(F32)
    last1 = one_ref[WIDTH + 8 : WIDTH + 9].astype(F32)
    last2 = two_ref[WIDTH + 8 : WIDTH + 9].astype(F32)
    near = jnp.where(last1 == u[:, :1].astype(F32), 1.0, 0.0)
    far = jnp.where(jnp.logical_and(first1 == last1, last2 == first1), near, 0.0)
    past = (1 + lax.broadcasted_iota(jnp.int32, (ROWS, HEAD), 0)).astype(F32)
    for i in range(STEP):
        h = step * STEP + i
        ld = log_decay(rate_ref, h)
        cols = slice(i * HEAD, (i + 1) * HEAD)
        rows = pl.ds(pl.multiple_of(h * HEAD, HEAD), HEAD)
        fade = jnp.exp(jnp.full((1, HEAD), ROWS * 1.0, F32) * ld) * far
        state = near * one_ref[rows].astype(F32) + fade * two_ref[rows].astype(F32)
        carried = jnp.dot(q_ref[:, cols], state.astype(BF16), preferred_element_type=F32)
        here = pl.ds(pl.multiple_of((step % 2) * COLS + i * HEAD, HEAD), HEAD)
        part = jnp.where(step < 2, part0_ref[:, here], part1_ref[:, here])
        kept = part + carried * (jnp.exp(past * ld) * open_ref[...])
        mean = jnp.mean(kept, axis=1, keepdims=True)
        centred = kept - mean
        variance = jnp.mean(centred * centred, axis=1, keepdims=True)
        normed = centred * lax.rsqrt(variance + 1e-05) * gain_ref[:, cols]
        a = a_ref[:, cols].astype(F32)
        out_ref[:, cols] = (a / (1.0 + jnp.exp(-a)) * normed).astype(BF16)


def shard_of(way, oc, y, z):
    (y0, z0), (y1, z1) = way
    dy, dz = y0 * (1 - oc) + y1 * oc, z0 * (1 - oc) + z1 * oc
    return ((y + dy + 2 * NY) % NY) * NZ + (z + dz + 2 * NZ) % NZ


def project_kernel(owner, g_ref, *refs):
    pieces, (out_ref, w_ref) = refs[:PIECES], refs[-2:]
    pack = lax.axis_index("pack")
    core = lax.axis_index("hist") % 2
    oc = core if owner == 0 else 1 - core
    y, z = pack // NZ, pack % NZ
    step = pl.program_id(0)

    @pl.when(step == 0)
    def _():
        for piece, ways in zip(pieces, SHARDS):
            for j, way in enumerate(ways):
                rows = pl.ds(pl.multiple_of(shard_of(way, oc, y, z) * 64, 64), 64)
                w_ref[rows] = piece[j * 64 : j * 64 + 64]

    cols = pl.ds(pl.multiple_of(step * 512, 512), 512)
    out_ref[...] = jnp.dot(g_ref[...], w_ref[:, cols], preferred_element_type=F32).astype(BF16)


SMALL = [
    [(0, 0), (-1, 0), (0, -4), (-1, -4), (-2, 0), (-3, 0), (-2, -4), (1, -4)],
    [(0, 0), (0, -1), (0, 1), (0, 2), (0, -2), (0, -3), (0, 3), (0, -4)],
]


def turned(d):
    both = [((y0, z0 + d), (y1 + d, z1)) for (y0, z0), (y1, z1) in zip(*SMALL)]
    return both[:4], both[4:]


SHARDS = [*turned(0), *turned(-1), *turned(1), turned(-2)[0], turned(2)[1]]
PIECES = len(SHARDS)


def moves(*ways):
    pairs = []
    for y in range(NY):
        for z in range(NZ):
            for h in range(NH):
                dy, dz = ways[h % 2]
                to = ((y + dy) % NY) * NZ + (z + dz) % NZ
                pairs.append(((y * NZ + z) * NH + h, to * NH + h))
    return pairs


def send(x, *ways):
    return lax.ppermute(x, BOTH, moves(*ways))


def swapped(x):
    return lax.ppermute(x, BOTH, [(i, i ^ 1) for i in range(NY * NZ * NH)])


def gather(w):
    core = lax.axis_index("hist") % 2
    x = lax.dynamic_slice_in_dim(w, core * 1024, 1024, 1)
    a1 = send(x, (1, 0), (0, 1))
    a2 = send(x, (0, 4), (0, -1))
    b1 = send(a1, (1, 0), (0, 1))
    b2 = send(a2, (1, 0), (0, -1))
    c1 = send(b1, (1, 0), (0, 1))
    c2 = send(b2, (1, 0), (0, -1))
    d1 = send(jnp.where(core == 0, a2, c1), (-1, 0), (0, 1))
    one = jnp.concatenate([x, a1, a2, b2], 0)
    two = jnp.concatenate([b1, c1, c2, d1], 0)
    up1 = send(one, (0, 1), (1, 0))
    down1 = send(one, (0, -1), (-1, 0))
    up2 = send(two, (0, 1), (1, 0))
    down2 = send(two, (0, -1), (-1, 0))
    far1 = send(up1, (0, 1), (1, 0))
    far2 = send(down2, (0, -1), (-1, 0))
    return one, two, up1, up2, down1, down2, far1, far2


def call(kernel, grid, in_specs, out_specs, out_shape, scratch, flops, nbytes, vmem=14, alias=None):
    return pl.pallas_call(
        kernel,
        grid_spec=pltpu.PrefetchScalarGridSpec(
            num_scalar_prefetch=0,
            grid=grid,
            in_specs=in_specs,
            out_specs=out_specs,
            scratch_shapes=scratch,
        ),
        out_shape=out_shape,
        cost_estimate=pl.CostEstimate(flops=flops, transcendentals=0, bytes_accessed=nbytes),
        compiler_params=pltpu.CompilerParams(vmem_limit_bytes=vmem << 20),
        input_output_aliases=alias or {},
    )


def local(queries, keys, values, gates, user_ids, forget_rate, norm_gain, w_out):
    q, k, v, a = (pltpu.with_memory_space_constraint(x[0], pltpu.HBM) for x in (queries, keys, values, gates))
    user_ids, forget_rate = (pltpu.with_memory_space_constraint(x, pltpu.HBM) for x in (user_ids, forget_rate))
    gain = norm_gain.reshape(1, WIDTH)
    steps = HEADS // STEP
    smem = pl.BlockSpec(memory_space=pltpu.SMEM)
    users = pl.BlockSpec((1, ROWS), lambda i: (0, 0))
    block = pl.BlockSpec((ROWS, COLS), lambda i: (0, i))
    heads = pl.BlockSpec((STEP, HEAD, HEAD), lambda i: (i, 0, 0))
    full = pl.BlockSpec((PAYLOAD, HEAD), lambda i: (0, 0))
    vmem = pl.BlockSpec(memory_space=pltpu.VMEM)
    shape = jax.ShapeDtypeStruct
    pay_shape = shape((PAYLOAD, HEAD), BF16)
    mb = 1 << 20

    pieces = gather(w_out)
    others = [swapped(p) for p in pieces]
    own, mid = call(
        state_kernel, (steps,), [smem, users, block, block], (full, heads),
        (pay_shape, shape((HEADS, HEAD, HEAD), BF16)),
        [pltpu.VMEM((2, HALF, HEAD), F32)], 270 * 10**6, 5 * mb,
    )(forget_rate, user_ids, k, v)
    one = lax.ppermute(own, "hist", [(i, i + 1) for i in range(NH - 1)])
    parts = []
    for i in range(2):

        def at(j, i=i):
            return 0, 2 * i + j

        half = pl.BlockSpec((ROWS, COLS), at)
        mids = pl.BlockSpec((STEP, HEAD, HEAD), lambda j, i=i: (2 * i + j, 0, 0))
        parts.append(
            call(
                functools.partial(inner_kernel, 2 * i), (2,), [smem, users, half, half, half, mids],
                block, shape((ROWS, WIDTH // 2), F32),
                [pltpu.VMEM((HALF, HALF), F32), pltpu.VMEM((2, HALF, HALF), F32), pltpu.VMEM((HALF, HEAD), F32)],
                600 * 10**6, 6 * mb,
            )(forget_rate, user_ids, q, k, v, mid)
        )
    pair = call(
        pair_kernel, (1,), [smem, users, vmem, vmem], vmem, pay_shape, [], 10**6, 3 * mb // 2
    )(forget_rate, user_ids, own, one)
    two = lax.ppermute(pair, "hist", [(i, i + 2) for i in range(NH - 2)])
    gated = call(
        gate_kernel, (steps,),
        [
            smem, users, vmem, vmem, block, vmem, vmem, block, pl.BlockSpec((1, COLS), lambda i: (0, i)),
        ],
        block, shape((ROWS, WIDTH), BF16), [pltpu.VMEM((ROWS, HEAD), F32)],
        300 * 10**6, 11 * mb,
    )(forget_rate, user_ids, one, two, q, *parts, a, gain)

    mixed = None
    for owner, got in enumerate((pieces, others)):

        def column(i, owner=owner):
            core = lax.axis_index("hist") % 2
            return 0, 2 * (core if owner == 0 else 1 - core) + i

        mixed = call(
            functools.partial(project_kernel, owner), (2,),
            [pl.BlockSpec(memory_space=pltpu.VMEM)] * (1 + PIECES) + [pl.BlockSpec(memory_space=pl.ANY)] * owner,
            pl.BlockSpec((ROWS, 512), column), shape((ROWS, WIDTH), BF16),
            [pltpu.VMEM((WIDTH, 1024), BF16)],
            2150 * 10**6, 7 * mb, 14, {1 + PIECES: 0} if owner else None,
        )(gated, *got, *([mixed] if owner else []))
    return mixed[None]


def solution(mesh):
    wide = P("pack", "hist", None)
    in_specs = (wide, wide, wide, wide, P("pack", "hist"), P(), P(), P("pack", None))
    return jax.shard_map(local, mesh=mesh, in_specs=in_specs, out_specs=wide, check_vma=False)
```
